512 devices in a mesh: gx: 32 (over x_hi, y, core), gy: 16 (over x_lo, z).
Axes of the slice: x: 4 (x_hi: 2, x_lo: 2; x = x_hi * 2 + x_lo), y: 8, z: 8, core: 2. Of those that a mesh axis runs over, the one named last changes fastest.
Arguments:
- rhs: float32 [32, 125, 2048], P('gx', None, 'gy'), may hold values from -6 to 6
- inverse: bfloat16 [32, 125, 125, 2048], P('gx', None, None, 'gy')
- weights: float32 [32, 4, 2048], P('gx', None, 'gy'), may hold values from 0.12 to 0.3
- neighbours: int32 [32, 4, 2048], P('gx', None, 'gy'), may hold values from 0 to 383, as said below
- send_lists: int32 [32, 4, 1024], P('gx', None, 'gy'), may hold values from 0 to 127
- coloring: int32 [32, 16], P('gx', 'gy'), may hold values from 0 to 3, as said below
Outputs:
- solution: float32 [32, 125, 2048], P('gx', None, 'gy')
- norms: float32 [2], replicated
The draws below stay inside these ranges and needn't reach their ends.
Inputs may be any that keep to these rules, and one draw needn't show every extreme that they name: `coloring`: the color of subdomain (i, j) depends only on i mod 2 and j mod 2, and the four parity classes have four different colors; which class has which color varies. `neighbours`: slots below 128 are the subdomain's own faces, the rest the received intersection faces in the order of the steps; every received slot is used by some face.
All inputs are finite; a program needn't handle non-finite values.
Results may differ from the reference program's by a relative error of at most 0.0055.
Values sent between devices are 32-bit elements; how exact they have to be, the bound alone decides.
A program may use at most 64 MiB of HBM per device.

```python
import math
import jax
import jax.numpy as jnp
from jax import lax

ROWS = 125
FACES = 128
HALO = 64
NEIGH = 4
SWEEPS = 2
N_GX = 32
N_GY = 16


def draw_inverse(key, part):
    first, second = jax.random.split(key)
    shape = (N_GX, ROWS, ROWS, N_GY * FACES)
    spread = 0.02 * jax.random.normal(first, shape, jnp.float32)
    diagonal = jax.random.uniform(second, (N_GX, 1, 1, N_GY * FACES), jnp.float32, 0.5, 0.9)
    unit = jnp.eye(ROWS, dtype=jnp.float32)[None, :, :, None]
    return (spread * (1.0 - unit) + unit * diagonal).astype(jnp.bfloat16)


def one_device(key):
    first, second = jax.random.split(key)
    order = jax.random.permutation(first, 2 * FACES).astype(jnp.int32)
    lead = jnp.stack([FACES + order[:FACES], FACES + order[FACES:]])
    rest = jax.random.randint(second, (NEIGH - 2, FACES), 0, 3 * FACES).astype(jnp.int32)
    return jnp.concatenate([lead, rest], axis=0)


def draw_neighbours(key, part):
    keys = jax.random.split(jax.random.fold_in(key, 7), N_GX * N_GY)
    tables = jax.vmap(one_device)(keys)
    tables = tables.reshape(N_GX, N_GY, NEIGH, FACES).transpose(0, 2, 1, 3)
    return tables.reshape(N_GX, NEIGH, N_GY * FACES).astype(jnp.int32)


def draw_coloring(key, part):
    order = jax.random.permutation(jax.random.fold_in(key, 11), 4).astype(jnp.int32)
    first = (jnp.arange(N_GX, dtype=jnp.int32) % 2)[:, None]
    second = (jnp.arange(N_GY, dtype=jnp.int32) % 2)[None, :]
    return order[first * 2 + second].astype(jnp.int32)


def plant(drawn, key, low, largest):
    spot = [jax.random.randint(jax.random.fold_in(key, axis), (), 0, length) for axis, length in enumerate(drawn.shape)]
    widest = drawn.shape.index(max(drawn.shape))
    neighbour = spot[:widest] + [(spot[widest] + 1) % drawn.shape[widest]] + spot[widest + 1:]
    return drawn.at[tuple(spot)].set(low).at[tuple(neighbour)].set(largest)


def level_of(key, shape, cuts, low, largest):
    factor_of, own = 1.0, jax.random.fold_in(key, 6)
    for dim, blocks in cuts:
        draws = jnp.exp(jax.random.uniform(jax.random.fold_in(own, dim), (blocks,), jnp.float32, low / len(cuts), largest / len(cuts)))
        factor_of = factor_of * jnp.repeat(draws, shape[dim] // blocks).reshape([-1 if axis == dim else 1 for axis in range(len(shape))])
    return factor_of


def normal_values(own_key, dims, scale, limit, shards=(), kind=jnp.bfloat16):
    result = scale * jax.random.normal(own_key, dims, jnp.float32)
    if shards:
        result = result * level_of(own_key, dims, shards, -0.22, 0.18)
    return jnp.clip(result, -limit, limit).astype(kind)


def setup_inputs(seed: int = 0) -> dict:
    seeds = jax.random.split(jax.random.key(seed), 7)
    return {
        "rhs": normal_values(seeds[0], (N_GX, ROWS, N_GY * FACES), 1.0, 6.0, ((0, 32), (2, 16)), jnp.float32),
        "inverse": draw_inverse(jax.random.fold_in(seeds[6], 71), 0),
        "weights": jnp.clip(jnp.exp(math.log(0.3) - 0.9162908 * jax.random.uniform(seeds[2], (N_GX, NEIGH, N_GY * FACES), jnp.float32) ** level_of(seeds[2], (N_GX, NEIGH, N_GY * FACES), ((0, 32), (2, 16)), -0.2, 0.2)), 0.12, 0.3),
        "neighbours": draw_neighbours(jax.random.fold_in(seeds[6], 71), 0),
        "send_lists": plant(jax.random.randint(seeds[4], (N_GX, 4, N_GY * HALO), 0, FACES), jax.random.fold_in(seeds[4], 1), 0, FACES - 1).astype(jnp.int32),
        "coloring": draw_coloring(jax.random.fold_in(seeds[6], 71), 0),
    }


def apply_rows(pair):
    block, source = pair
    return jnp.einsum('ijyf,jyf->iyf', block.astype(jnp.float32), source.astype(jnp.float32))

def reference(rhs, inverse, weights, neighbours, send_lists, coloring):
    halo_faces = FACES // 2
    right = rhs.reshape(N_GX, ROWS, N_GY, FACES)
    coupling = weights.reshape(N_GX, NEIGH, N_GY, FACES)
    slots = neighbours.reshape(N_GX, NEIGH, N_GY, FACES)
    sending = send_lists.reshape(N_GX, 4, N_GY, halo_faces)
    blocks = inverse.reshape(N_GX, ROWS, ROWS, N_GY, FACES)
    solution = jnp.zeros((N_GX, ROWS, N_GY, FACES), jnp.float32)
    zero_rows = jnp.zeros((1, ROWS, N_GY, halo_faces), jnp.float32)
    zero_cols = jnp.zeros((N_GX, ROWS, 1, halo_faces), jnp.float32)
    results = []
    for sweep in range(SWEEPS):
        squares = jnp.zeros((), jnp.float32)
        for color in range(4):
            packs = []
            for side in range(4):
                index = jnp.broadcast_to(sending[:, side][:, None], (N_GX, ROWS, N_GY, halo_faces))
                packs.append(jnp.take_along_axis(solution, index, axis=3))
            below = jnp.concatenate([zero_rows, packs[0][:-1]], axis=0)
            above = jnp.concatenate([packs[1][1:], zero_rows], axis=0)
            left = jnp.concatenate([zero_cols, packs[2][:, :, :-1]], axis=2)
            right_side = jnp.concatenate([packs[3][:, :, 1:], zero_cols], axis=2)
            extended = jnp.concatenate([solution, below, above, left, right_side], axis=3)
            couple = jnp.zeros_like(solution)
            for k in range(NEIGH):
                index = jnp.broadcast_to(slots[:, k][:, None], (N_GX, ROWS, N_GY, FACES))
                couple = couple + coupling[:, k][:, None] * jnp.take_along_axis(extended, index, axis=3)
            source = (right + couple).astype(jnp.bfloat16)
            candidate = lax.map(apply_rows, (blocks, source))
            active = (coloring == color)[:, None, :, None]
            delta = jnp.where(active, candidate - solution, 0.0)
            squares = squares + jnp.sum(delta * delta)
            solution = jnp.where(active, candidate, solution)
        results.append(jnp.sqrt(squares))
    return (solution.reshape(N_GX, ROWS, N_GY * FACES), jnp.stack(results))
```

```python
import functools

import jax
import jax.numpy as jnp
from jax import lax
from jax.experimental import pallas as pl
from jax.experimental.pallas import tpu as pltpu
from jax.sharding import PartitionSpec as P

MESH = pl.DeviceIdType.MESH
ROWS, FACES, HALO, SIDES = 125, 128, 64, 4
N_GX, N_GY = 32, 16
GROUP_A, GROUP_B = 16, 32
F32 = jnp.float32


def gather(x, index):
    return jnp.take_along_axis(x, index, axis=1, mode="promise_in_bounds")


def total(values):
    while len(values) > 1:
        values = [a + b for a, b in zip(values[::2], values[1::2])] + (
            [values[-1]] if len(values) % 2 else []
        )
    return values[0]


def row_sums(acc, sub):
    def merge(a, b, rows, shift):
        mine = functools.reduce(
            jnp.logical_or, [sub == r for r in rows]
        )
        return jnp.where(mine, a, b) + pltpu.roll(jnp.where(mine, b, a), shift, axis=0)

    x1 = merge(acc[0], acc[4], (0, 5, 6, 7), 4)
    x2 = merge(acc[2], acc[6], (0, 1, 2, 7), 4)
    x3 = merge(acc[1], acc[5], (0, 1, 6, 7), 4)
    x4 = merge(acc[3], acc[7], (0, 1, 2, 3), 4)
    y1 = merge(x1, x2, (0, 3, 4, 7), 2)
    y2 = merge(x3, x4, (0, 1, 4, 5), 2)
    return merge(y1, y2, (0, 2, 4, 6), 1)


def kernel(
    levels,
    rounds,
    color_ref,
    rhs_ref,
    inv_hbm,
    w_ref,
    nb_ref,
    sl_ref,
    out_ref,
    norm_ref,
    stage,
    inv,
    base,
    src,
    sol,
    own,
    lane_of,
    weight_of,
    pick_of,
    send_buf,
    halo_buf,
    squares,
    part_a,
    part_b,
    buf_a,
    buf_b,
    load_sem,
    send_sem,
    recv_sem,
    send_a,
    recv_a,
    send_b,
    recv_b,
):
    gx, gy = lax.axis_index("gx"), lax.axis_index("gy")
    core, y, x_hi = gx % 2, (gx // 2) % 8, gx // 16
    z, x_lo = gy % 8, gy // 8
    me_a = core * 8 + z
    me_b = (x_hi * 2 + x_lo) * 8 + y

    def device_a(q):
        return (gx - core + q // 8, gy - z + q % 8)

    def device_b(q):
        x, other = q // 8, q % 8
        return ((x // 2) * 16 + other * 2 + core, (x % 2) * 8 + z)

    has = (gx > 0, gx < N_GX - 1, gy > 0, gy < N_GY - 1)
    to = (gx < N_GX - 1, gx > 0, gy < N_GY - 1, gy > 0)
    receiver = ((gx + 1, gy), (gx - 1, gy), (gx, gy + 1), (gx, gy - 1))

    def load(piece):
        start = (piece // 2) * 16 + (piece % 2) * 64
        size = min(16, ROWS - start)
        return pltpu.make_async_copy(
            inv_hbm.at[pl.ds(start, size)], stage.at[pl.ds(start, size)], load_sem.at[piece]
        )

    for piece in range(8):
        load(piece).start()

    barrier = pltpu.get_barrier_semaphore()
    for d in range(SIDES):
        @pl.when(to[d])
        def _():
            pl.semaphore_signal(barrier, inc=1, device_id=receiver[d], device_id_type=MESH)

    def greet(group, me, device):
        def step(q, carry):
            @pl.when(q != me)
            def _():
                pl.semaphore_signal(barrier, inc=1, device_id=device(q), device_id_type=MESH)
            return carry
        lax.fori_loop(0, group, step, 0)

    greet(GROUP_A, me_a, device_a)
    greet(GROUP_B, me_b, device_b)

    lane = lax.broadcasted_iota(jnp.int32, (8, FACES), 1)
    sub = lax.broadcasted_iota(jnp.int32, (8, FACES), 0)
    low = lane < HALO
    zero = jnp.zeros((8, FACES), F32)
    color = jnp.full((8, FACES), color_ref[0, 0], jnp.int32)

    for d in range(SIDES):
        @pl.when(jnp.logical_not(has[d]))
        def _():
            for t in range(rounds - 1):
                halo_buf[t, d] = jnp.zeros((HALO, FACES), F32)

    for k in range(4):
        slot = jnp.broadcast_to(nb_ref[k : k + 1, :], (8, FACES))
        strength = jnp.broadcast_to(w_ref[k : k + 1, :], (8, FACES))
        lane_of[k] = slot % FACES
        lane_of[4 + k] = (slot % FACES + HALO) % FACES
        for part in range(3):
            weight_of[part * 4 + k] = jnp.where(slot // FACES == part, strength, 0.0)
    for d in range(SIDES):
        faces = jnp.broadcast_to(sl_ref[d : d + 1, :], (8, HALO))
        pick_of[d, :, 0:HALO] = faces
        pick_of[d, :, HALO:FACES] = faces

    base[pl.ds(120, 8), :] = zero
    base[pl.ds(0, ROWS), :] = rhs_ref[...]
    src[...] = base[...].astype(jnp.bfloat16).astype(F32)
    sol[...] = jnp.zeros((FACES, FACES), F32)
    squares[...] = jnp.zeros((2, 8, FACES), F32)

    def clear(r, carry):
        inv[r, pl.ds(120, 8), :] = zero
        return carry
    lax.fori_loop(0, ROWS, clear, 0)
    inv[pl.ds(ROWS, 3)] = jnp.zeros((3, FACES, FACES), F32)

    def product(block, sources):
        acc = []
        for j in range(8):
            row = block * 8 + j
            acc.append(total([inv[row, pl.ds(8 * i, 8), :] * sources[i] for i in range(16)]))
        return row_sums(acc, sub)

    def accepted(t):
        first, second = levels
        return color_in(first, t), color_in(second, t)

    def color_in(table, t):
        mask = None
        for c in range(4):
            hit = jnp.logical_and(color == c, jnp.full((8, FACES), t, jnp.int32) == table[c])
            mask = hit if mask is None else jnp.logical_or(mask, hit)
        return mask

    def rounds_body(t, lo, hi, pack):
        now_1, now_2 = accepted(t)
        take = jnp.logical_or(now_1, now_2)
        sources = [src[pl.ds(8 * i, 8), :] for i in range(16)]

        def step(v, dd):
            news = []
            for block in (v, v + 8):
                at = pl.ds(pl.multiple_of(block * 8, 8), 8)
                old = sol[at, :]
                candidate = product(block, sources)
                delta = jnp.where(take, candidate - old, 0.0)
                new = jnp.where(take, candidate, old)
                sol[at, :] = new
                news.append(new)
                dd = dd + delta * delta
            if pack:
                at = pl.ds(pl.multiple_of(v * 8, 8), 8)
                for d in range(SIDES):
                    here = gather(news[0], pick_of[d])
                    there = gather(news[1], pick_of[d])
                    parts = (here, there) if d % 2 == 0 else (there, here)
                    send_buf[t - 1, d, at, :] = jnp.where(low, parts[0], parts[1])
            return dd

        dd = lax.fori_loop(lo, hi, step, zero)
        squares[0] += jnp.where(now_1, dd, 0.0)
        squares[1] += jnp.where(now_2, dd, 0.0)

    def copy(t, d):
        return pltpu.make_async_remote_copy(
            src_ref=send_buf.at[t - 1, d],
            dst_ref=halo_buf.at[t - 1, d],
            send_sem=send_sem.at[t - 1, d],
            recv_sem=recv_sem.at[t - 1, d],
            device_id=receiver[d],
            device_id_type=MESH,
        )

    def send(t):
        for d in range(SIDES):
            @pl.when(to[d])
            def _():
                copy(t, d).start()

    def own_part():
        for v in range(16):
            at = pl.ds(8 * v, 8)
            mine = sol[at, :]
            terms = [weight_of[k] * gather(mine, lane_of[k]) for k in range(4)]
            own[at, :] = base[at, :] + total(terms)

    def receive(t, pair):
        for d in (2 * pair, 2 * pair + 1):
            @pl.when(has[d])
            def _():
                copy(t, d).wait_recv()

    def halo_part(t, pair, final):
        for v in range(8):
            at = pl.ds(8 * v, 8)
            before = halo_buf[t - 1, 2 * pair, at, :]
            after = halo_buf[t - 1, 2 * pair + 1, at, :]
            for half in range(2):
                where = pl.ds(8 * v + 64 * half, 8)
                both = jnp.where(low, before, after) if half == 0 else jnp.where(low, after, before)
                terms = [
                    weight_of[4 + 4 * pair + k] * gather(both, lane_of[4 * half + k])
                    for k in range(4)
                ]
                value = own[where, :] + total(terms)
                if final:
                    src[where, :] = value.astype(jnp.bfloat16).astype(F32)
                else:
                    own[where, :] = value

    for q in range(4):
        for piece in (2 * q, 2 * q + 1):
            load(piece).wait()
            start = (piece // 2) * 16 + (piece % 2) * 64
            size = min(16, ROWS - start)

            def widen(r, carry):
                inv[r, pl.ds(0, ROWS), :] = stage[r].astype(F32)
                return carry
            lax.fori_loop(start, start + size, widen, 0)
        rounds_body(1, 2 * q, 2 * q + 2, True)

    beside = jnp.minimum(gx, 1) + jnp.minimum(N_GX - 1 - gx, 1)
    beside += jnp.minimum(gy, 1) + jnp.minimum(N_GY - 1 - gy, 1)
    pl.semaphore_wait(barrier, beside + (GROUP_A - 1 + GROUP_B - 1))

    send(1)
    own_part()

    def middle(t, carry):
        for pair in range(2):
            receive(t - 1, pair)
            halo_part(t - 1, pair, pair == 1)
        rounds_body(t, 0, 8, True)
        send(t)
        own_part()
        return carry
    lax.fori_loop(2, rounds, middle, 0)

    for pair in range(2):
        receive(rounds - 1, pair)
        halo_part(rounds - 1, pair, pair == 1)
    rounds_body(rounds, 0, 8, False)

    def exchange(value, part, buf, group, me, device, send_s, recv_s):
        part[...] = value
        buf[me] = value

        def copy_to(q):
            return pltpu.make_async_remote_copy(
                src_ref=part,
                dst_ref=buf.at[me],
                send_sem=send_s.at[q],
                recv_sem=recv_s.at[me],
                device_id=device(q),
                device_id_type=MESH,
            )

        def copy_from(q):
            return pltpu.make_async_remote_copy(
                src_ref=part,
                dst_ref=buf.at[q],
                send_sem=send_s.at[q],
                recv_sem=recv_s.at[q],
                device_id=device(q),
                device_id_type=MESH,
            )

        def others(act):
            def step(q, carry):
                @pl.when(q != me)
                def _():
                    act(q)
                return carry
            lax.fori_loop(0, group, step, 0)

        others(lambda q: copy_to(q).start())
        return others, copy_to, copy_from

    mine = jnp.concatenate(
        [jnp.sum(squares[0], axis=0, keepdims=True), jnp.sum(squares[1], axis=0, keepdims=True)], axis=0
    )
    others_a, to_a, from_a = exchange(mine, part_a, buf_a, GROUP_A, me_a, device_a, send_a, recv_a)
    out_ref[...] = sol[pl.ds(0, ROWS), :]
    others_a(lambda q: from_a(q).wait_recv())
    line = total([buf_a[q] for q in range(GROUP_A)])
    others_b, to_b, from_b = exchange(line, part_b, buf_b, GROUP_B, me_b, device_b, send_b, recv_b)
    for d in range(SIDES):
        @pl.when(to[d])
        def _():
            def step(t, carry):
                copy(t, d).wait_send()
                return carry
            lax.fori_loop(1, rounds, step, 0)
    others_a(lambda q: to_a(q).wait_send())
    others_b(lambda q: from_b(q).wait_recv())
    whole = jnp.sum(total([buf_b[q] for q in range(GROUP_B)]), axis=1, keepdims=True)
    norm_ref[...] = jnp.broadcast_to(jnp.sqrt(whole), (2, FACES))
    others_b(lambda q: to_b(q).wait_send())


def sweep_call(levels, rounds, collective_id):
    vmem, dma = pltpu.VMEM, pltpu.SemaphoreType.DMA
    square = vmem((FACES, FACES), F32)
    whole = pl.BlockSpec(memory_space=pltpu.VMEM)
    return pl.pallas_call(
        functools.partial(kernel, levels, rounds),
        out_shape=(
            jax.ShapeDtypeStruct((ROWS, FACES), F32),
            jax.ShapeDtypeStruct((2, FACES), F32),
        ),
        in_specs=[
            pl.BlockSpec(memory_space=pltpu.SMEM),
            whole,
            pl.BlockSpec(memory_space=pl.ANY),
            whole,
            whole,
            whole,
        ],
        out_specs=(whole, whole),
        scratch_shapes=[
            vmem((ROWS, ROWS, FACES), jnp.bfloat16),
            vmem((FACES, FACES, FACES), F32),
            square,
            square,
            square,
            square,
            vmem((8, 8, FACES), jnp.int32),
            vmem((12, 8, FACES), F32),
            vmem((SIDES, 8, FACES), jnp.int32),
            vmem((rounds - 1, SIDES, HALO, FACES), F32),
            vmem((rounds - 1, SIDES, HALO, FACES), F32),
            vmem((2, 8, FACES), F32),
            vmem((2, FACES), F32),
            vmem((2, FACES), F32),
            vmem((GROUP_A, 2, FACES), F32),
            vmem((GROUP_B, 2, FACES), F32),
            dma((8,)),
            dma((rounds - 1, SIDES)),
            dma((rounds - 1, SIDES)),
            dma((GROUP_A,)),
            dma((GROUP_A,)),
            dma((GROUP_B,)),
            dma((GROUP_B,)),
        ],
        compiler_params=pltpu.CompilerParams(
            collective_id=collective_id, has_side_effects=True
        ),
    )


CHAIN = ((1, 2, 3, 4), (5, 6, 7, 8))


def body(rhs, inverse, weights, neighbours, send_lists, coloring):
    solved, norms = sweep_call(CHAIN, 8, 0)(
        coloring, rhs[0], inverse[0], weights[0], neighbours[0], send_lists[0]
    )
    return solved[None], norms[:, 0]


def solution(mesh):
    in_specs = (
        P("gx", None, "gy"),
        P("gx", None, None, "gy"),
        P("gx", None, "gy"),
        P("gx", None, "gy"),
        P("gx", None, "gy"),
        P("gx", "gy"),
    )
    out_specs = (P("gx", None, "gy"), P())
    return jax.shard_map(body, mesh=mesh, in_specs=in_specs, out_specs=out_specs, check_vma=False)
```

```python
import functools

import jax
import jax.numpy as jnp
from jax import lax
from jax.experimental import pallas as pl
from jax.experimental.pallas import tpu as pltpu
from jax.sharding import PartitionSpec as P

MESH = pl.DeviceIdType.MESH
ROWS, FACES, HALO, SIDES = 125, 128, 64, 4
N_GX, N_GY = 32, 16
F32 = jnp.float32


def gather(x, index):
    return jnp.take_along_axis(x, index, axis=1, mode="promise_in_bounds")


def total(values):
    while len(values) > 1:
        values = [a + b for a, b in zip(values[::2], values[1::2])] + (
            [values[-1]] if len(values) % 2 else []
        )
    return values[0]


def row_sums(acc, sub):
    def merge(a, b, rows, shift):
        mine = functools.reduce(
            jnp.logical_or, [sub == r for r in rows]
        )
        return jnp.where(mine, a, b) + pltpu.roll(jnp.where(mine, b, a), shift, axis=0)

    x1 = merge(acc[0], acc[4], (0, 5, 6, 7), 4)
    x2 = merge(acc[2], acc[6], (0, 1, 2, 7), 4)
    x3 = merge(acc[1], acc[5], (0, 1, 6, 7), 4)
    x4 = merge(acc[3], acc[7], (0, 1, 2, 3), 4)
    y1 = merge(x1, x2, (0, 3, 4, 7), 2)
    y2 = merge(x3, x4, (0, 1, 4, 5), 2)
    return merge(y1, y2, (0, 2, 4, 6), 1)


def kernel(
    levels,
    rounds,
    color_ref,
    rhs_ref,
    inv_hbm,
    w_ref,
    nb_ref,
    sl_ref,
    out_ref,
    norm_ref,
    stage,
    inv,
    base,
    src,
    sol,
    own,
    lane_of,
    weight_of,
    pick_of,
    send_buf,
    halo_buf,
    squares,
    part_a,
    part_b,
    buf_a,
    buf_b,
    load_sem,
    send_sem,
    recv_sem,
    line_sem,
    hello,
):
    gx, gy = lax.axis_index("gx"), lax.axis_index("gy")
    has = (gx > 0, gx < N_GX - 1, gy > 0, gy < N_GY - 1)
    to = (gx < N_GX - 1, gx > 0, gy < N_GY - 1, gy > 0)
    receiver = ((gx + 1, gy), (gx - 1, gy), (gx, gy + 1), (gx, gy - 1))

    load = pltpu.make_async_copy(inv_hbm, stage, load_sem)
    load.start()

    barrier = pltpu.get_barrier_semaphore()
    for d in range(SIDES):
        @pl.when(to[d])
        def _():
            pl.semaphore_signal(barrier, inc=1, device_id=receiver[d], device_id_type=MESH)

    def far(step, axis):
        here, count = ((gx, N_GX), (gy, N_GY))[axis]
        place = (lambda at: (at, gy)) if axis == 0 else (lambda at: (gx, at))
        back, ahead = here >= step, here < count - step
        return (back, place(here - step)), (ahead, place(here + step))

    def meet(step, slot, axes):
        for axis in axes:
            for there, device in far(step, axis):
                @pl.when(there)
                def _():
                    pl.semaphore_signal(hello.at[slot], inc=1, device_id=device, device_id_type=MESH)

    def met(step, slot, axes):
        peers = 0
        for axis in axes:
            here, count = ((gx, N_GX), (gy, N_GY))[axis]
            peers += jnp.minimum(here // step, 1) + jnp.minimum((count - 1 - here) // step, 1)
        pl.semaphore_wait(hello.at[slot], peers)

    def widen_circle(t):
        if t == 2:
            meet(2, 0, (0, 1))
        elif t == 3:
            met(2, 0, (0, 1))
            meet(4, 1, (0, 1))
        elif t == 4:
            met(4, 1, (0, 1))
            meet(8, 2, (1,))
            meet(8, 3, (0,))

    lane = lax.broadcasted_iota(jnp.int32, (8, FACES), 1)
    sub = lax.broadcasted_iota(jnp.int32, (8, FACES), 0)
    low = lane < HALO
    zero = jnp.zeros((8, FACES), F32)
    color = jnp.full((8, FACES), color_ref[0, 0], jnp.int32)

    for d in range(SIDES):
        @pl.when(jnp.logical_not(has[d]))
        def _():
            for slot in range(2):
                halo_buf[slot, d] = jnp.zeros((HALO, FACES), F32)

    for k in range(4):
        slot = jnp.broadcast_to(nb_ref[k : k + 1, :], (8, FACES))
        strength = jnp.broadcast_to(w_ref[k : k + 1, :], (8, FACES))
        lane_of[k] = slot % FACES
        lane_of[4 + k] = (slot % FACES + HALO) % FACES
        for part in range(3):
            weight_of[part * 4 + k] = jnp.where(slot // FACES == part, strength, 0.0)
    for d in range(SIDES):
        faces = jnp.broadcast_to(sl_ref[d : d + 1, :], (8, HALO))
        pick_of[d, :, 0:HALO] = faces
        pick_of[d, :, HALO:FACES] = faces

    base[pl.ds(120, 8), :] = zero
    base[pl.ds(0, ROWS), :] = rhs_ref[...]
    src[...] = base[...].astype(jnp.bfloat16).astype(F32)
    sol[...] = jnp.zeros((FACES, FACES), F32)
    squares[...] = jnp.zeros((2, 8, FACES), F32)

    def clear(r, carry):
        inv[r, pl.ds(120, 8), :] = zero
        return carry
    lax.fori_loop(0, ROWS, clear, 0)
    inv[pl.ds(ROWS, 3)] = jnp.zeros((3, FACES, FACES), F32)

    def product(block, sources):
        acc = []
        for j in range(8):
            row = block * 8 + j
            acc.append(total([inv[row, pl.ds(8 * i, 8), :] * sources[i] for i in range(16)]))
        return row_sums(acc, sub)

    def accepted(t):
        first, second = levels
        return color_in(first, t), color_in(second, t)

    def color_in(table, t):
        mask = None
        for c in range(4):
            hit = jnp.logical_and(color == c, jnp.full((8, FACES), t, jnp.int32) == table[c])
            mask = hit if mask is None else jnp.logical_or(mask, hit)
        return mask

    def rounds_body(t, lo, hi, pack):
        now_1, now_2 = accepted(t)
        take = jnp.logical_or(now_1, now_2)
        sources = [src[pl.ds(8 * i, 8), :] for i in range(16)]

        def step(v, dd):
            news = []
            for block in (v, v + 8):
                at = pl.ds(pl.multiple_of(block * 8, 8), 8)
                old = sol[at, :]
                candidate = product(block, sources)
                delta = jnp.where(take, candidate - old, 0.0)
                new = jnp.where(take, candidate, old)
                sol[at, :] = new
                news.append(new)
                dd = dd + delta * delta
            if pack:
                at = pl.ds(pl.multiple_of(v * 8, 8), 8)
                for d in range(SIDES):
                    here = gather(news[0], pick_of[d])
                    there = gather(news[1], pick_of[d])
                    parts = (here, there) if d % 2 == 0 else (there, here)
                    send_buf[t % 2, d, at, :] = jnp.where(low, parts[0], parts[1])
            return dd

        dd = lax.fori_loop(lo, hi, step, zero)
        squares[0] += jnp.where(now_1, dd, 0.0)
        squares[1] += jnp.where(now_2, dd, 0.0)

    def copy(t, d):
        return pltpu.make_async_remote_copy(
            src_ref=send_buf.at[t % 2, d],
            dst_ref=halo_buf.at[t % 2, d],
            send_sem=send_sem.at[t % 2, d],
            recv_sem=recv_sem.at[t % 2, d],
            device_id=receiver[d],
            device_id_type=MESH,
        )

    def send(t):
        for d in range(SIDES):
            @pl.when(to[d])
            def _():
                copy(t, d).start()

    def sent(t):
        for d in range(SIDES):
            @pl.when(to[d])
            def _():
                copy(t, d).wait_send()

    def own_part():
        for v in range(16):
            at = pl.ds(8 * v, 8)
            mine = sol[at, :]
            terms = [weight_of[k] * gather(mine, lane_of[k]) for k in range(4)]
            own[at, :] = base[at, :] + total(terms)

    def receive(t, pair):
        for d in (2 * pair, 2 * pair + 1):
            @pl.when(has[d])
            def _():
                copy(t, d).wait_recv()

    def halo_part(t, pair, final):
        for v in range(8):
            at = pl.ds(8 * v, 8)
            before = halo_buf[t % 2, 2 * pair, at, :]
            after = halo_buf[t % 2, 2 * pair + 1, at, :]
            for half in range(2):
                where = pl.ds(8 * v + 64 * half, 8)
                both = jnp.where(low, before, after) if half == 0 else jnp.where(low, after, before)
                terms = [
                    weight_of[4 + 4 * pair + k] * gather(both, lane_of[4 * half + k])
                    for k in range(4)
                ]
                value = own[where, :] + total(terms)
                if final:
                    src[where, :] = value.astype(jnp.bfloat16).astype(F32)
                else:
                    own[where, :] = value

    load.wait()

    def widen(r, carry):
        inv[r, pl.ds(0, ROWS), :] = stage[r].astype(F32)
        return carry
    lax.fori_loop(0, ROWS, widen, 0)
    rounds_body(1, 0, 8, True)

    beside = jnp.minimum(gx, 1) + jnp.minimum(N_GX - 1 - gx, 1)
    beside += jnp.minimum(gy, 1) + jnp.minimum(N_GY - 1 - gy, 1)
    pl.semaphore_wait(barrier, beside)

    send(1)
    own_part()

    def gather_halos(t):
        for pair in range(2):
            receive(t - 1, pair)
            halo_part(t - 1, pair, pair == 1)

    def middle(t, carry):
        gather_halos(t)
        for early in (2, 3, 4):
            if early < rounds:
                @pl.when(t == early)
                def _():
                    widen_circle(early)
        @pl.when(t > 2)
        def _():
            sent(t - 2)
        rounds_body(t, 0, 8, True)
        send(t)
        own_part()
        return carry
    lax.fori_loop(2, rounds, middle, 0)

    gather_halos(rounds)
    widen_circle(rounds)
    rounds_body(rounds, 0, 8, False)

    def exchange(value, part, buf, group, me, device, first_sem):
        part[...] = value
        buf[me] = value

        def to_all(q, carry):
            @pl.when(q != me)
            def _():
                pltpu.make_async_remote_copy(
                    src_ref=part,
                    dst_ref=buf.at[me],
                    send_sem=line_sem.at[first_sem],
                    recv_sem=line_sem.at[first_sem + 1],
                    device_id=device(q),
                    device_id_type=MESH,
                ).start()
            return carry
        lax.fori_loop(0, group, to_all, 0)

        def wait(which):
            every = buf.at[pl.ds(0, group - 1)]
            pltpu.make_async_copy(every, every, line_sem.at[first_sem + which]).wait()
        return wait

    mine = jnp.concatenate(
        [jnp.sum(squares[0], axis=0, keepdims=True), jnp.sum(squares[1], axis=0, keepdims=True)], axis=0
    )
    met(8, 2, (1,))
    wait_a = exchange(mine, part_a, buf_a, N_GY, gy, lambda q: (gx, q), 0)
    met(8, 3, (0,))
    meet(16, 4, (0,))
    out_ref[...] = sol[pl.ds(0, ROWS), :]
    sent(rounds - 2)
    sent(rounds - 1)
    wait_a(1)
    line = total([buf_a[q] for q in range(N_GY)])
    met(16, 4, (0,))
    wait_b = exchange(line, part_b, buf_b, N_GX, gx, lambda q: (q, gy), 2)
    wait_a(0)
    wait_b(1)
    whole = jnp.sum(total([buf_b[q] for q in range(N_GX)]), axis=1, keepdims=True)
    norm_ref[...] = jnp.broadcast_to(jnp.sqrt(whole), (2, FACES))
    wait_b(0)


def sweep_call(levels, rounds, collective_id):
    vmem, dma = pltpu.VMEM, pltpu.SemaphoreType.DMA
    square = vmem((FACES, FACES), F32)
    whole = pl.BlockSpec(memory_space=pltpu.VMEM)
    return pl.pallas_call(
        functools.partial(kernel, levels, rounds),
        out_shape=(
            jax.ShapeDtypeStruct((ROWS, FACES), F32),
            jax.ShapeDtypeStruct((2, FACES), F32),
        ),
        in_specs=[
            pl.BlockSpec(memory_space=pltpu.SMEM),
            whole,
            pl.BlockSpec(memory_space=pl.ANY),
            whole,
            whole,
            whole,
        ],
        out_specs=(whole, whole),
        scratch_shapes=[
            vmem((ROWS, ROWS, FACES), jnp.bfloat16),
            vmem((FACES, FACES, FACES), F32),
            square,
            square,
            square,
            square,
            vmem((8, 8, FACES), jnp.int32),
            vmem((12, 8, FACES), F32),
            vmem((SIDES, 8, FACES), jnp.int32),
            vmem((2, SIDES, HALO, FACES), F32),
            vmem((2, SIDES, HALO, FACES), F32),
            vmem((2, 8, FACES), F32),
            vmem((2, FACES), F32),
            vmem((2, FACES), F32),
            vmem((N_GY, 2, FACES), F32),
            vmem((N_GX, 2, FACES), F32),
            dma,
            dma((2, SIDES)),
            dma((2, SIDES)),
            dma((4,)),
            pltpu.SemaphoreType.REGULAR((5,)),
        ],
        compiler_params=pltpu.CompilerParams(
            collective_id=collective_id, has_side_effects=True
        ),
    )


PLANS = (
    (((1, 1, 2, 2), (3, 3, 4, 4)), 4),
    (((1, 2, 2, 3), (3, 4, 4, 5)), 5),
    (((1, 2, 3, 4), (5, 6, 7, 8)), 8),
)
DIAGONAL = [(i * N_GY + j, (i ^ 1) * N_GY + (j ^ 1)) for i in range(N_GX) for j in range(N_GY)]


def body(rhs, inverse, weights, neighbours, send_lists, coloring):
    across = lax.ppermute(coloring, ("gx", "gy"), DIAGONAL)[0, 0] ^ coloring[0, 0]
    plan = jnp.where(across == 1, 0, jnp.where(across == 3, 1, 2))
    solved, norms = lax.switch(
        plan,
        [sweep_call(*choice, number) for number, choice in enumerate(PLANS)],
        coloring, rhs[0], inverse[0], weights[0], neighbours[0], send_lists[0],
    )
    return solved[None], norms[:, 0]


def solution(mesh):
    in_specs = (
        P("gx", None, "gy"),
        P("gx", None, None, "gy"),
        P("gx", None, "gy"),
        P("gx", None, "gy"),
        P("gx", None, "gy"),
        P("gx", "gy"),
    )
    out_specs = (P("gx", None, "gy"), P())
    return jax.shard_map(body, mesh=mesh, in_specs=in_specs, out_specs=out_specs, check_vma=False)
```

```python
import functools

import jax
import jax.numpy as jnp
from jax import lax
from jax.experimental import pallas as pl
from jax.experimental.pallas import tpu as pltpu
from jax.sharding import PartitionSpec as P

MESH = pl.DeviceIdType.MESH
ROWS, FACES, HALO, SIDES = 125, 128, 64, 4
N_GX, N_GY = 32, 16
F32 = jnp.float32


def gather(x, index):
    return jnp.take_along_axis(x, index, axis=1, mode="promise_in_bounds")


def total(values):
    while len(values) > 1:
        values = [a + b for a, b in zip(values[::2], values[1::2])] + (
            [values[-1]] if len(values) % 2 else []
        )
    return values[0]


def row_sums(acc, sub):
    def merge(a, b, rows, shift):
        mine = functools.reduce(
            jnp.logical_or, [sub == r for r in rows]
        )
        return jnp.where(mine, a, b) + pltpu.roll(jnp.where(mine, b, a), shift, axis=0)

    x1 = merge(acc[0], acc[4], (0, 5, 6, 7), 4)
    x2 = merge(acc[2], acc[6], (0, 1, 2, 7), 4)
    x3 = merge(acc[1], acc[5], (0, 1, 6, 7), 4)
    x4 = merge(acc[3], acc[7], (0, 1, 2, 3), 4)
    y1 = merge(x1, x2, (0, 3, 4, 7), 2)
    y2 = merge(x3, x4, (0, 1, 4, 5), 2)
    return merge(y1, y2, (0, 2, 4, 6), 1)


def product(inv, block, sources, sub):
    acc = []
    for j in range(8):
        row = block * 8 + j
        acc.append(total([inv[row, pl.ds(8 * i, 8), :] * sources[i] for i in range(16)]))
    return row_sums(acc, sub)


def pad(inv):
    zero = jnp.zeros((8, FACES), F32)

    def clear(r, carry):
        inv[r, pl.ds(120, 8), :] = zero
        return carry
    lax.fori_loop(0, ROWS, clear, 0)
    inv[pl.ds(ROWS, 3)] = jnp.zeros((3, FACES, FACES), F32)


def widen(stage, inv, lo, hi):
    def step(r, carry):
        inv[r, pl.ds(0, ROWS), :] = stage[r].astype(F32)
        return carry
    lax.fori_loop(lo, hi, step, 0)


def beside(gx, gy):
    has = (gx > 0, gx < N_GX - 1, gy > 0, gy < N_GY - 1)
    to = (gx < N_GX - 1, gx > 0, gy < N_GY - 1, gy > 0)
    receiver = ((gx + 1, gy), (gx - 1, gy), (gx, gy + 1), (gx, gy - 1))
    return has, to, receiver


def peers(here, count, step):
    return jnp.minimum(here // step, 1) + jnp.minimum((count - 1 - here) // step, 1)


def set_picks(pick_of, sl_ref):
    for d in range(SIDES):
        faces = jnp.broadcast_to(sl_ref[d : d + 1, :], (8, HALO))
        pick_of[d, :, 0:HALO] = faces
        pick_of[d, :, HALO:FACES] = faces


def packed(d, upper, lower, pick_of, low):
    here = gather(upper, pick_of[d])
    there = gather(lower, pick_of[d])
    return jnp.where(low, here, there) if d % 2 == 0 else jnp.where(low, there, here)


def first_kernel(
    color_ref, rhs_ref, inv_hbm, sl_ref, plan_ref, out_ref, inv, halo_ref,
    stage, base, pick_of, send_buf, recv_buf, load_sem, send_sem, recv_sem,
):
    gx, gy = lax.axis_index("gx"), lax.axis_index("gy")
    has, to, receiver = beside(gx, gy)
    barrier = pltpu.get_barrier_semaphore()
    for d in range(SIDES):
        @pl.when(to[d])
        def _():
            pl.semaphore_signal(barrier, inc=1, device_id=receiver[d], device_id_type=MESH)

    def load(piece):
        rows = pl.ds(32 * piece, min(32, ROWS - 32 * piece))
        return pltpu.make_async_copy(inv_hbm.at[rows], stage.at[rows], load_sem.at[piece])

    for piece in range(4):
        load(piece).start()
    sub = lax.broadcasted_iota(jnp.int32, (8, FACES), 0)
    low = lax.broadcasted_iota(jnp.int32, (8, FACES), 1) < HALO
    own = color_ref[0, 0]
    for d in range(SIDES):
        send_buf[d, pl.ds(HALO, 8), :] = jnp.full((8, FACES), own, jnp.int32).astype(F32)

        @pl.when(jnp.logical_not(has[d]))
        def _():
            recv_buf[d] = jnp.zeros((HALO + 8, FACES), F32)
    set_picks(pick_of, sl_ref)
    base[pl.ds(120, 8), :] = jnp.zeros((8, FACES), F32)
    base[pl.ds(0, ROWS), :] = rhs_ref[...].reshape(ROWS, FACES)
    pad(inv)
    base[...] = base[...].astype(jnp.bfloat16).astype(F32)
    for piece in range(4):
        load(piece).wait()
        widen(stage, inv, 32 * piece, min(32 * piece + 32, ROWS))

        def step(block, carry):
            sources = [base[pl.ds(8 * i, 8), :] for i in range(16)]
            out_ref[pl.ds(pl.multiple_of(block * 8, 8), 8), :] = product(inv, block, sources, sub)
            return carry
        lax.fori_loop(4 * piece, 4 * piece + 4, step, 0)
    for v in range(8):
        upper, lower = out_ref[pl.ds(8 * v, 8), :], out_ref[pl.ds(8 * v + HALO, 8), :]
        for d in range(SIDES):
            send_buf[d, pl.ds(8 * v, 8), :] = packed(d, upper, lower, pick_of, low)
    pl.semaphore_wait(barrier, peers(gx, N_GX, 1) + peers(gy, N_GY, 1))

    def copy(d):
        return pltpu.make_async_remote_copy(
            src_ref=send_buf.at[d],
            dst_ref=recv_buf.at[d],
            send_sem=send_sem.at[d],
            recv_sem=recv_sem.at[d],
            device_id=receiver[d],
            device_id_type=MESH,
        )

    for d in range(SIDES):
        @pl.when(to[d])
        def _():
            copy(d).start()
    for d in range(SIDES):
        @pl.when(has[d])
        def _():
            copy(d).wait_recv()

    colors = [recv_buf[d, pl.ds(HALO, 8), :] for d in range(SIDES)]
    near = jnp.maximum(colors[0], colors[1]) + jnp.maximum(colors[2], colors[3])
    early = jnp.logical_or(near == 1.0, near == 5.0)
    for d in range(SIDES):
        moved = jnp.logical_or(colors[d] == 0.0, jnp.logical_and(colors[d] == 1.0, early))
        for v in range(8):
            halo_ref[d, pl.ds(8 * v, 8), :] = jnp.where(moved, recv_buf[d, pl.ds(8 * v, 8), :], 0.0)
    across = own ^ (6 - own - jnp.max(near).astype(jnp.int32))
    plan_ref[0, 0] = jnp.where(across == 1, 0, jnp.where(across == 3, 1, 2))
    for d in range(SIDES):
        @pl.when(to[d])
        def _():
            copy(d).wait_send()


def kernel(
    levels,
    rounds,
    color_ref,
    rhs_ref,
    first_ref,
    inv,
    first_halo,
    w_ref,
    nb_ref,
    sl_ref,
    out_ref,
    norm_ref,
    base,
    src,
    sol,
    own,
    lane_of,
    weight_of,
    pick_of,
    send_buf,
    halo_buf,
    squares,
    part_a,
    part_b,
    buf_a,
    buf_b,
    send_sem,
    recv_sem,
    line_sem,
    hello,
):
    gx, gy = lax.axis_index("gx"), lax.axis_index("gy")
    has, to, receiver = beside(gx, gy)

    barrier = pltpu.get_barrier_semaphore()

    def far(step, axis):
        here, count = ((gx, N_GX), (gy, N_GY))[axis]
        place = (lambda at: (at, gy)) if axis == 0 else (lambda at: (gx, at))
        back, ahead = here >= step, here < count - step
        return (back, place(here - step)), (ahead, place(here + step))

    def greet(step, semaphore, axes):
        for axis in axes:
            for there, device in far(step, axis):
                @pl.when(there)
                def _():
                    pl.semaphore_signal(semaphore, inc=1, device_id=device, device_id_type=MESH)

    def around(step, axes):
        places = ((gx, N_GX), (gy, N_GY))
        return sum(peers(*places[axis], step) for axis in axes)

    def meet(step, slot, axes):
        greet(step, hello.at[slot], axes)

    def met(step, slot, axes):
        pl.semaphore_wait(hello.at[slot], around(step, axes))

    def widen_circle(t):
        if t == 3:
            met(2, 0, (0, 1))
            meet(4, 1, (0, 1))
        elif t == 4:
            met(4, 1, (0, 1))
            meet(8, 2, (1,))
            meet(8, 3, (0,))

    greet(1, barrier, (0, 1))
    greet(2, barrier, (0, 1))

    lane = lax.broadcasted_iota(jnp.int32, (8, FACES), 1)
    sub = lax.broadcasted_iota(jnp.int32, (8, FACES), 0)
    low = lane < HALO
    zero = jnp.zeros((8, FACES), F32)
    color = jnp.full((8, FACES), color_ref[0, 0], jnp.int32)

    for d in range(SIDES):
        @pl.when(jnp.logical_not(has[d]))
        def _():
            for slot in range(2):
                halo_buf[slot, d] = jnp.zeros((HALO, FACES), F32)

    for k in range(4):
        slot = jnp.broadcast_to(nb_ref[k : k + 1, :], (8, FACES))
        strength = jnp.broadcast_to(w_ref[k : k + 1, :], (8, FACES))
        lane_of[k] = slot % FACES
        lane_of[4 + k] = (slot % FACES + HALO) % FACES
        for part in range(3):
            weight_of[part * 4 + k] = jnp.where(slot // FACES == part, strength, 0.0)
    set_picks(pick_of, sl_ref)

    base[pl.ds(120, 8), :] = zero
    base[pl.ds(0, ROWS), :] = rhs_ref[...].reshape(ROWS, FACES)
    sol[...] = jnp.zeros((FACES, FACES), F32)
    squares[...] = jnp.zeros((2, 8, FACES), F32)

    def accepted(t):
        first, second = levels
        return color_in(first, t), color_in(second, t)

    def color_in(table, t):
        mask = None
        for c in range(4):
            hit = jnp.logical_and(color == c, jnp.full((8, FACES), t, jnp.int32) == table[c])
            mask = hit if mask is None else jnp.logical_or(mask, hit)
        return mask

    def rounds_body(t, lo, hi, pack, ready=None):
        now_1, now_2 = accepted(t)
        take = jnp.logical_or(now_1, now_2)
        sources = [src[pl.ds(8 * i, 8), :] for i in range(16)] if ready is None else None

        def step(v, dd):
            news = []
            for block in (v, v + 8):
                at = pl.ds(pl.multiple_of(block * 8, 8), 8)
                old = sol[at, :]
                candidate = product(inv, block, sources, sub) if ready is None else ready[at, :]
                delta = jnp.where(take, candidate - old, 0.0)
                new = jnp.where(take, candidate, old)
                sol[at, :] = new
                news.append(new)
                dd = dd + delta * delta
            if pack:
                at = pl.ds(pl.multiple_of(v * 8, 8), 8)
                for d in range(SIDES):
                    send_buf[t % 2, d, at, :] = packed(d, *news, pick_of, low)
            return dd

        dd = lax.fori_loop(lo, hi, step, zero)
        squares[0] += jnp.where(now_1, dd, 0.0)
        squares[1] += jnp.where(now_2, dd, 0.0)

    def copy(t, d):
        return pltpu.make_async_remote_copy(
            src_ref=send_buf.at[t % 2, d],
            dst_ref=halo_buf.at[t % 2, d],
            send_sem=send_sem.at[t % 2, d],
            recv_sem=recv_sem.at[t % 2, d],
            device_id=receiver[d],
            device_id_type=MESH,
        )

    def send(t):
        for d in range(SIDES):
            @pl.when(to[d])
            def _():
                copy(t, d).start()

    def sent(t):
        for d in range(SIDES):
            @pl.when(to[d])
            def _():
                copy(t, d).wait_send()

    def own_part():
        for v in range(16):
            at = pl.ds(8 * v, 8)
            mine = sol[at, :]
            terms = [weight_of[k] * gather(mine, lane_of[k]) for k in range(4)]
            own[at, :] = base[at, :] + total(terms)

    def receive(t, pair):
        for d in (2 * pair, 2 * pair + 1):
            @pl.when(has[d])
            def _():
                copy(t, d).wait_recv()

    def halo_part(halos, pair, final):
        for v in range(8):
            at = pl.ds(8 * v, 8)
            before = halos[2 * pair, at, :]
            after = halos[2 * pair + 1, at, :]
            for half in range(2):
                where = pl.ds(8 * v + 64 * half, 8)
                both = jnp.where(low, before, after) if half == 0 else jnp.where(low, after, before)
                terms = [
                    weight_of[4 + 4 * pair + k] * gather(both, lane_of[4 * half + k])
                    for k in range(4)
                ]
                value = own[where, :] + total(terms)
                if final:
                    src[where, :] = value.astype(jnp.bfloat16).astype(F32)
                else:
                    own[where, :] = value

    rounds_body(1, 0, 8, False, first_ref)
    own_part()

    for pair in range(2):
        halo_part(first_halo, pair, pair == 1)
    rounds_body(2, 0, 8, True)
    pl.semaphore_wait(barrier, around(1, (0, 1)) + around(2, (0, 1)))
    send(2)
    meet(2, 0, (0, 1))
    own_part()

    def gather_halos(t):
        for pair in range(2):
            receive(t - 1, pair)
            halo_part(halo_buf.at[(t - 1) % 2], pair, pair == 1)

    def middle(t, carry):
        gather_halos(t)
        for early in (3, 4):
            if early < rounds:
                @pl.when(t == early)
                def _():
                    widen_circle(early)
        @pl.when(t > 3)
        def _():
            sent(t - 2)
        rounds_body(t, 0, 8, True)
        send(t)
        own_part()
        return carry
    lax.fori_loop(3, rounds, middle, 0)

    gather_halos(rounds)
    widen_circle(rounds)
    rounds_body(rounds, 0, 8, False)

    def exchange(value, part, buf, group, me, device, first_sem):
        part[...] = value
        buf[me] = value

        def to(offset, carry):
            pltpu.make_async_remote_copy(
                src_ref=part,
                dst_ref=buf.at[me],
                send_sem=line_sem.at[first_sem],
                recv_sem=line_sem.at[first_sem + 1],
                device_id=device((me + offset) % group),
                device_id_type=MESH,
            ).start()
            return carry
        lax.fori_loop(group // 2, group, to, 0)
        lax.fori_loop(1, group // 2, to, 0)

        def wait(which):
            every = buf.at[pl.ds(0, group - 1)]
            pltpu.make_async_copy(every, every, line_sem.at[first_sem + which]).wait()
        return wait

    mine = jnp.concatenate(
        [jnp.sum(squares[0], axis=0, keepdims=True), jnp.sum(squares[1], axis=0, keepdims=True)], axis=0
    )
    met(8, 2, (1,))
    wait_a = exchange(mine, part_a, buf_a, N_GY, gy, lambda q: (gx, q), 0)
    met(8, 3, (0,))
    meet(16, 4, (0,))
    out_ref[...] = sol[pl.ds(0, ROWS), :]
    sent(rounds - 2)
    sent(rounds - 1)
    wait_a(1)
    line = total([buf_a[q] for q in range(N_GY)])
    met(16, 4, (0,))
    wait_b = exchange(line, part_b, buf_b, N_GX, gx, lambda q: (q, gy), 2)
    wait_a(0)
    wait_b(1)
    whole = jnp.sum(total([buf_b[q] for q in range(N_GX)]), axis=1, keepdims=True)
    norm_ref[...] = jnp.broadcast_to(jnp.sqrt(whole), (2, FACES))
    wait_b(0)


def first_call(collective_id):
    vmem, dma = pltpu.VMEM, pltpu.SemaphoreType.DMA
    smem = pl.BlockSpec(memory_space=pltpu.SMEM)
    whole = pl.BlockSpec(memory_space=pltpu.VMEM)
    return pl.pallas_call(
        first_kernel,
        out_shape=(
            jax.ShapeDtypeStruct((1, 1), jnp.int32),
            jax.ShapeDtypeStruct((FACES, FACES), F32),
            jax.ShapeDtypeStruct((FACES, FACES, FACES), F32),
            jax.ShapeDtypeStruct((SIDES, HALO, FACES), F32),
        ),
        in_specs=[smem, whole, pl.BlockSpec(memory_space=pl.ANY), whole],
        out_specs=(smem, whole, whole, whole),
        scratch_shapes=[
            vmem((ROWS, ROWS, FACES), jnp.bfloat16),
            vmem((FACES, FACES), F32),
            vmem((SIDES, 8, FACES), jnp.int32),
            vmem((SIDES, HALO + 8, FACES), F32),
            vmem((SIDES, HALO + 8, FACES), F32),
            dma((4,)),
            dma((SIDES,)),
            dma((SIDES,)),
        ],
        compiler_params=pltpu.CompilerParams(
            collective_id=collective_id, has_side_effects=True, vmem_limit_bytes=54 * 2**20
        ),
    )


def sweep_call(levels, rounds, collective_id):
    vmem, dma = pltpu.VMEM, pltpu.SemaphoreType.DMA
    square = vmem((FACES, FACES), F32)
    whole = pl.BlockSpec(memory_space=pltpu.VMEM)
    return pl.pallas_call(
        functools.partial(kernel, levels, rounds),
        out_shape=(
            jax.ShapeDtypeStruct((ROWS, FACES), F32),
            jax.ShapeDtypeStruct((2, FACES), F32),
        ),
        in_specs=[
            pl.BlockSpec(memory_space=pltpu.SMEM),
            whole,
            whole,
            whole,
            whole,
            whole,
            whole,
            whole,
        ],
        out_specs=(whole, whole),
        scratch_shapes=[
            square,
            square,
            square,
            square,
            vmem((8, 8, FACES), jnp.int32),
            vmem((12, 8, FACES), F32),
            vmem((SIDES, 8, FACES), jnp.int32),
            vmem((2, SIDES, HALO, FACES), F32),
            vmem((2, SIDES, HALO, FACES), F32),
            vmem((2, 8, FACES), F32),
            vmem((2, FACES), F32),
            vmem((2, FACES), F32),
            vmem((N_GY, 2, FACES), F32),
            vmem((N_GX, 2, FACES), F32),
            dma((2, SIDES)),
            dma((2, SIDES)),
            dma((4,)),
            pltpu.SemaphoreType.REGULAR((5,)),
        ],
        compiler_params=pltpu.CompilerParams(
            collective_id=collective_id, has_side_effects=True, vmem_limit_bytes=24 * 2**20
        ),
    )


PLANS = (
    (((1, 1, 2, 2), (3, 3, 4, 4)), 4),
    (((1, 2, 2, 3), (3, 4, 4, 5)), 5),
    (((1, 2, 3, 4), (5, 6, 7, 8)), 8),
)


def body(rhs, inverse, weights, neighbours, send_lists, coloring):
    right = jnp.transpose(rhs, (1, 0, 2))
    plan, first, wide, halos = first_call(len(PLANS))(coloring, right, inverse[0], send_lists[0])
    solved, norms = lax.switch(
        plan[0, 0],
        [sweep_call(*choice, number) for number, choice in enumerate(PLANS)],
        coloring, right, first, wide, halos, weights[0], neighbours[0], send_lists[0],
    )
    return solved[None], norms[:, 0]


def solution(mesh):
    in_specs = (
        P("gx", None, "gy"),
        P("gx", None, None, "gy"),
        P("gx", None, "gy"),
        P("gx", None, "gy"),
        P("gx", None, "gy"),
        P("gx", "gy"),
    )
    out_specs = (P("gx", None, "gy"), P())
    return jax.shard_map(body, mesh=mesh, in_specs=in_specs, out_specs=out_specs, check_vma=False)
```

```python
import functools

import jax
import jax.numpy as jnp
from jax import lax
from jax.experimental import pallas as pl
from jax.experimental.pallas import tpu as pltpu
from jax.sharding import PartitionSpec as P

MESH = pl.DeviceIdType.MESH
ROWS, FACES, HALO, SIDES = 125, 128, 64, 4
N_GX, N_GY = 32, 16
F32 = jnp.float32


def gather(x, index):
    return jnp.take_along_axis(x, index, axis=1, mode="promise_in_bounds")


def total(values):
    while len(values) > 1:
        values = [a + b for a, b in zip(values[::2], values[1::2])] + (
            [values[-1]] if len(values) % 2 else []
        )
    return values[0]


def row_sums(acc, sub):
    def merge(a, b, rows, shift):
        mine = functools.reduce(
            jnp.logical_or, [sub == r for r in rows]
        )
        return jnp.where(mine, a, b) + pltpu.roll(jnp.where(mine, b, a), shift, axis=0)

    x1 = merge(acc[0], acc[4], (0, 5, 6, 7), 4)
    x2 = merge(acc[2], acc[6], (0, 1, 2, 7), 4)
    x3 = merge(acc[1], acc[5], (0, 1, 6, 7), 4)
    x4 = merge(acc[3], acc[7], (0, 1, 2, 3), 4)
    y1 = merge(x1, x2, (0, 3, 4, 7), 2)
    y2 = merge(x3, x4, (0, 1, 4, 5), 2)
    return merge(y1, y2, (0, 2, 4, 6), 1)


def product(inv, block, sources, sub):
    acc = []
    for j in range(8):
        row = block * 8 + j
        acc.append(total([inv[row, pl.ds(8 * i, 8), :] * sources[i] for i in range(16)]))
    return row_sums(acc, sub)


def pad(inv):
    zero = jnp.zeros((8, FACES), F32)

    def clear(r, carry):
        inv[r, pl.ds(120, 8), :] = zero
        return carry
    lax.fori_loop(0, ROWS, clear, 0)
    inv[pl.ds(ROWS, 3)] = jnp.zeros((3, FACES, FACES), F32)


def widen(stage, inv, lo, hi):
    def step(r, carry):
        inv[r, pl.ds(0, ROWS), :] = stage[r].astype(F32)
        return carry
    lax.fori_loop(lo, hi, step, 0)


def beside(gx, gy):
    has = (gx > 0, gx < N_GX - 1, gy > 0, gy < N_GY - 1)
    to = (gx < N_GX - 1, gx > 0, gy < N_GY - 1, gy > 0)
    receiver = ((gx + 1, gy), (gx - 1, gy), (gx, gy + 1), (gx, gy - 1))
    return has, to, receiver


def peers(here, count, step):
    return jnp.minimum(here // step, 1) + jnp.minimum((count - 1 - here) // step, 1)


def set_picks(pick_of, sl_ref):
    for d in range(SIDES):
        faces = jnp.broadcast_to(sl_ref[d : d + 1, :], (8, HALO))
        pick_of[d, :, 0:HALO] = faces
        pick_of[d, :, HALO:FACES] = faces


def packed(d, upper, lower, pick_of, low):
    here = gather(upper, pick_of[d])
    there = gather(lower, pick_of[d])
    return jnp.where(low, here, there) if d % 2 == 0 else jnp.where(low, there, here)


def first_kernel(
    color_ref, rhs_ref, inv_hbm, sl_ref, plan_ref, out_ref, inv, halo_ref,
    stage, base, pick_of, send_buf, recv_buf, load_sem, send_sem, recv_sem,
):
    gx, gy = lax.axis_index("gx"), lax.axis_index("gy")
    has, to, receiver = beside(gx, gy)
    barrier = pltpu.get_barrier_semaphore()
    for d in range(SIDES):
        @pl.when(to[d])
        def _():
            pl.semaphore_signal(barrier, inc=1, device_id=receiver[d], device_id_type=MESH)

    def load(piece):
        rows = pl.ds(32 * piece, min(32, ROWS - 32 * piece))
        return pltpu.make_async_copy(inv_hbm.at[rows], stage.at[rows], load_sem.at[piece])

    for piece in range(4):
        load(piece).start()
    sub = lax.broadcasted_iota(jnp.int32, (8, FACES), 0)
    low = lax.broadcasted_iota(jnp.int32, (8, FACES), 1) < HALO
    own = color_ref[0, 0]
    for d in range(SIDES):
        send_buf[d, pl.ds(HALO, 8), :] = jnp.full((8, FACES), own, jnp.int32).astype(F32)

        @pl.when(jnp.logical_not(has[d]))
        def _():
            recv_buf[d] = jnp.zeros((HALO + 8, FACES), F32)
    set_picks(pick_of, sl_ref)
    base[pl.ds(120, 8), :] = jnp.zeros((8, FACES), F32)
    base[pl.ds(0, ROWS), :] = rhs_ref[...].reshape(ROWS, FACES)
    pad(inv)
    base[...] = base[...].astype(jnp.bfloat16).astype(F32)
    for piece in range(4):
        load(piece).wait()
        widen(stage, inv, 32 * piece, min(32 * piece + 32, ROWS))

        def step(block, carry):
            sources = [base[pl.ds(8 * i, 8), :] for i in range(16)]
            out_ref[pl.ds(pl.multiple_of(block * 8, 8), 8), :] = product(inv, block, sources, sub)
            return carry
        lax.fori_loop(4 * piece, 4 * piece + 4, step, 0)
    for v in range(8):
        upper, lower = out_ref[pl.ds(8 * v, 8), :], out_ref[pl.ds(8 * v + HALO, 8), :]
        for d in range(SIDES):
            send_buf[d, pl.ds(8 * v, 8), :] = packed(d, upper, lower, pick_of, low)
    pl.semaphore_wait(barrier, peers(gx, N_GX, 1) + peers(gy, N_GY, 1))

    def copy(d):
        return pltpu.make_async_remote_copy(
            src_ref=send_buf.at[d],
            dst_ref=recv_buf.at[d],
            send_sem=send_sem.at[d],
            recv_sem=recv_sem.at[d],
            device_id=receiver[d],
            device_id_type=MESH,
        )

    for d in range(SIDES):
        @pl.when(to[d])
        def _():
            copy(d).start()
    for d in range(SIDES):
        @pl.when(has[d])
        def _():
            copy(d).wait_recv()

    colors = [recv_buf[d, pl.ds(HALO, 8), :] for d in range(SIDES)]
    near_x = jnp.maximum(colors[0], colors[1])
    near = near_x + jnp.maximum(colors[2], colors[3])
    early = jnp.logical_or(near == 1.0, near == 5.0)
    for d in range(SIDES):
        moved = jnp.logical_or(colors[d] == 0.0, jnp.logical_and(colors[d] == 1.0, early))
        for v in range(8):
            halo_ref[d, pl.ds(8 * v, 8), :] = jnp.where(moved, recv_buf[d, pl.ds(8 * v, 8), :], 0.0)
    across = own ^ (6 - own - jnp.max(near).astype(jnp.int32))
    chain = jnp.where(own ^ jnp.max(near_x).astype(jnp.int32) == 1, 2, 3)
    plan_ref[0, 0] = jnp.where(across == 1, 0, jnp.where(across == 3, 1, chain))
    for d in range(SIDES):
        @pl.when(to[d])
        def _():
            copy(d).wait_send()


def kernel(
    levels,
    rounds,
    axis_01,
    color_ref,
    rhs_ref,
    first_ref,
    inv,
    first_halo,
    w_ref,
    nb_ref,
    sl_ref,
    out_ref,
    norm_ref,
    base,
    src,
    sol,
    own,
    lane_of,
    weight_of,
    pick_of,
    send_buf,
    halo_buf,
    squares,
    part_a,
    part_b,
    buf_a,
    buf_b,
    send_sem,
    recv_sem,
    line_sem,
    hello,
):
    gx, gy = lax.axis_index("gx"), lax.axis_index("gy")
    has, to, receiver = beside(gx, gy)

    barrier = pltpu.get_barrier_semaphore()

    def far(step, axis):
        here, count = ((gx, N_GX), (gy, N_GY))[axis]
        place = (lambda at: (at, gy)) if axis == 0 else (lambda at: (gx, at))
        back, ahead = here >= step, here < count - step
        return (back, place(here - step)), (ahead, place(here + step))

    def greet(step, semaphore, axes):
        for axis in axes:
            for there, device in far(step, axis):
                @pl.when(there)
                def _():
                    pl.semaphore_signal(semaphore, inc=1, device_id=device, device_id_type=MESH)

    def around(step, axes):
        places = ((gx, N_GX), (gy, N_GY))
        return sum(peers(*places[axis], step) for axis in axes)

    def meet(step, slot, axes):
        greet(step, hello.at[slot], axes)

    def met(step, slot, axes):
        pl.semaphore_wait(hello.at[slot], around(step, axes))

    def widen_circle(t):
        if t == 3:
            met(2, 0, (0, 1))
            meet(4, 1, (0, 1))
        elif t == 4:
            met(4, 1, (0, 1))
            meet(8, 2, (1,))
            meet(8, 3, (0,))

    greet(1, barrier, (0, 1))
    greet(2, barrier, (0, 1))

    lane = lax.broadcasted_iota(jnp.int32, (8, FACES), 1)
    sub = lax.broadcasted_iota(jnp.int32, (8, FACES), 0)
    low = lane < HALO
    zero = jnp.zeros((8, FACES), F32)
    color = jnp.full((8, FACES), color_ref[0, 0], jnp.int32)

    for d in range(SIDES):
        @pl.when(jnp.logical_not(has[d]))
        def _():
            for slot in range(2):
                halo_buf[slot, d] = jnp.zeros((HALO, FACES), F32)

    for k in range(4):
        slot = jnp.broadcast_to(nb_ref[k : k + 1, :], (8, FACES))
        strength = jnp.broadcast_to(w_ref[k : k + 1, :], (8, FACES))
        lane_of[k] = slot % FACES
        lane_of[4 + k] = (slot % FACES + HALO) % FACES
        for part in range(3):
            weight_of[part * 4 + k] = jnp.where(slot // FACES == part, strength, 0.0)
    set_picks(pick_of, sl_ref)

    base[pl.ds(120, 8), :] = zero
    base[pl.ds(0, ROWS), :] = rhs_ref[...].reshape(ROWS, FACES)
    sol[...] = jnp.zeros((FACES, FACES), F32)
    squares[...] = jnp.zeros((2, 8, FACES), F32)

    def accepted(t):
        first, second = levels
        return color_in(first, t), color_in(second, t)

    def color_in(table, t):
        mask = None
        for c in range(4):
            hit = jnp.logical_and(color == c, jnp.full((8, FACES), t, jnp.int32) == table[c])
            mask = hit if mask is None else jnp.logical_or(mask, hit)
        return mask

    def slot(t):
        return t % 2 if axis_01 is None else (t // 2) % 2

    def sides(t_parity):
        if axis_01 is None:
            return (0, 1, 2, 3)
        axis = axis_01 if t_parity % 2 else 1 - axis_01
        return (2 * axis, 2 * axis + 1)

    def rounds_body(t, lo, hi, pack, ready=None):
        now_1, now_2 = accepted(t)
        take = jnp.logical_or(now_1, now_2)
        sources = [src[pl.ds(8 * i, 8), :] for i in range(16)] if ready is None else None

        def step(v, dd):
            news = []
            for block in (v, v + 8):
                at = pl.ds(pl.multiple_of(block * 8, 8), 8)
                old = sol[at, :]
                candidate = product(inv, block, sources, sub) if ready is None else ready[at, :]
                delta = jnp.where(take, candidate - old, 0.0)
                new = jnp.where(take, candidate, old)
                sol[at, :] = new
                news.append(new)
                dd = dd + delta * delta
            if pack:
                at = pl.ds(pl.multiple_of(v * 8, 8), 8)
                for d in pack:
                    send_buf[slot(t), d, at, :] = packed(d, *news, pick_of, low)
            return dd

        dd = lax.fori_loop(lo, hi, step, zero)
        squares[0] += jnp.where(now_1, dd, 0.0)
        squares[1] += jnp.where(now_2, dd, 0.0)

    def copy(t, d):
        return pltpu.make_async_remote_copy(
            src_ref=send_buf.at[slot(t), d],
            dst_ref=halo_buf.at[slot(t), d],
            send_sem=send_sem.at[slot(t), d],
            recv_sem=recv_sem.at[slot(t), d],
            device_id=receiver[d],
            device_id_type=MESH,
        )

    def send(t, which):
        for d in which:
            @pl.when(to[d])
            def _():
                copy(t, d).start()

    def sent(t, which):
        for d in which:
            @pl.when(to[d])
            def _():
                copy(t, d).wait_send()

    def own_part():
        for v in range(16):
            at = pl.ds(8 * v, 8)
            mine = sol[at, :]
            terms = [weight_of[k] * gather(mine, lane_of[k]) for k in range(4)]
            own[at, :] = base[at, :] + total(terms)

    def receive(t, pair):
        for d in (2 * pair, 2 * pair + 1):
            @pl.when(has[d])
            def _():
                copy(t, d).wait_recv()

    def halo_part(halos, pair, final):
        for v in range(8):
            at = pl.ds(8 * v, 8)
            before = halos[2 * pair, at, :]
            after = halos[2 * pair + 1, at, :]
            for half in range(2):
                where = pl.ds(8 * v + 64 * half, 8)
                both = jnp.where(low, before, after) if half == 0 else jnp.where(low, after, before)
                terms = [
                    weight_of[4 + 4 * pair + k] * gather(both, lane_of[4 * half + k])
                    for k in range(4)
                ]
                value = own[where, :] + total(terms)
                if final:
                    src[where, :] = value.astype(jnp.bfloat16).astype(F32)
                else:
                    own[where, :] = value

    rounds_body(1, 0, 8, (), first_ref)
    own_part()

    for pair in range(2):
        halo_part(first_halo, pair, pair == 1)
    rounds_body(2, 0, 8, sides(2))
    pl.semaphore_wait(barrier, around(1, (0, 1)) + around(2, (0, 1)))
    send(2, sides(2))
    meet(2, 0, (0, 1))
    own_part()

    def gather_halos(t, parity):
        if axis_01 is None:
            for pair in range(2):
                receive(t - 1, pair)
                halo_part(halo_buf.at[slot(t - 1)], pair, pair == 1)
        else:
            new = sides(parity - 1)[0] // 2
            old = first_halo if isinstance(t, int) and t == 3 else halo_buf.at[slot(t - 2)]
            halo_part(old, 1 - new, False)
            receive(t - 1, new)
            halo_part(halo_buf.at[slot(t - 1)], new, True)

    reuse = 2 if axis_01 is None else 4

    def whole_round(t, parity):
        gather_halos(t, parity)
        for early in (3, 4):
            if early < rounds:
                @pl.when(t == early)
                def _():
                    widen_circle(early)
        @pl.when(t > 1 + reuse)
        def _():
            sent(t - reuse, sides(parity))
        rounds_body(t, 0, 8, sides(parity))
        send(t, sides(parity))
        own_part()

    if axis_01 is None:
        def middle(t, carry):
            whole_round(t, 0)
            return carry
        lax.fori_loop(3, rounds, middle, 0)
    else:
        whole_round(3, 1)

        def two(u, carry):
            whole_round(2 * u, 0)
            whole_round(2 * u + 1, 1)
            return carry
        lax.fori_loop(2, rounds // 2, two, 0)

    gather_halos(rounds, rounds)
    widen_circle(rounds)
    rounds_body(rounds, 0, 8, ())

    def exchange(value, part, buf, group, me, device, first_sem):
        part[...] = value
        buf[me] = value

        def to(offset, carry):
            pltpu.make_async_remote_copy(
                src_ref=part,
                dst_ref=buf.at[me],
                send_sem=line_sem.at[first_sem],
                recv_sem=line_sem.at[first_sem + 1],
                device_id=device((me + offset) % group),
                device_id_type=MESH,
            ).start()
            return carry
        lax.fori_loop(group // 2, group, to, 0)
        lax.fori_loop(1, group // 2, to, 0)

        def wait(which):
            every = buf.at[pl.ds(0, group - 1)]
            pltpu.make_async_copy(every, every, line_sem.at[first_sem + which]).wait()
        return wait

    mine = jnp.concatenate(
        [jnp.sum(squares[0], axis=0, keepdims=True), jnp.sum(squares[1], axis=0, keepdims=True)], axis=0
    )
    met(8, 2, (1,))
    wait_a = exchange(mine, part_a, buf_a, N_GY, gy, lambda q: (gx, q), 0)
    met(8, 3, (0,))
    meet(16, 4, (0,))
    out_ref[...] = sol[pl.ds(0, ROWS), :]
    for t in range(rounds - reuse, rounds):
        sent(t, sides(t))
    wait_a(1)
    line = total([buf_a[q] for q in range(N_GY)])
    met(16, 4, (0,))
    wait_b = exchange(line, part_b, buf_b, N_GX, gx, lambda q: (q, gy), 2)
    wait_a(0)
    wait_b(1)
    whole = jnp.sum(total([buf_b[q] for q in range(N_GX)]), axis=1, keepdims=True)
    norm_ref[...] = jnp.broadcast_to(jnp.sqrt(whole), (2, FACES))
    wait_b(0)


def first_call(collective_id):
    vmem, dma = pltpu.VMEM, pltpu.SemaphoreType.DMA
    smem = pl.BlockSpec(memory_space=pltpu.SMEM)
    whole = pl.BlockSpec(memory_space=pltpu.VMEM)
    return pl.pallas_call(
        first_kernel,
        out_shape=(
            jax.ShapeDtypeStruct((1, 1), jnp.int32),
            jax.ShapeDtypeStruct((FACES, FACES), F32),
            jax.ShapeDtypeStruct((FACES, FACES, FACES), F32),
            jax.ShapeDtypeStruct((SIDES, HALO, FACES), F32),
        ),
        in_specs=[smem, whole, pl.BlockSpec(memory_space=pl.ANY), whole],
        out_specs=(smem, whole, whole, whole),
        scratch_shapes=[
            vmem((ROWS, ROWS, FACES), jnp.bfloat16),
            vmem((FACES, FACES), F32),
            vmem((SIDES, 8, FACES), jnp.int32),
            vmem((SIDES, HALO + 8, FACES), F32),
            vmem((SIDES, HALO + 8, FACES), F32),
            dma((4,)),
            dma((SIDES,)),
            dma((SIDES,)),
        ],
        compiler_params=pltpu.CompilerParams(
            collective_id=collective_id, has_side_effects=True, vmem_limit_bytes=54 * 2**20
        ),
    )


def sweep_call(levels, rounds, axis_01, collective_id):
    vmem, dma = pltpu.VMEM, pltpu.SemaphoreType.DMA
    square = vmem((FACES, FACES), F32)
    whole = pl.BlockSpec(memory_space=pltpu.VMEM)
    return pl.pallas_call(
        functools.partial(kernel, levels, rounds, axis_01),
        out_shape=(
            jax.ShapeDtypeStruct((ROWS, FACES), F32),
            jax.ShapeDtypeStruct((2, FACES), F32),
        ),
        in_specs=[
            pl.BlockSpec(memory_space=pltpu.SMEM),
            whole,
            whole,
            whole,
            whole,
            whole,
            whole,
            whole,
        ],
        out_specs=(whole, whole),
        scratch_shapes=[
            square,
            square,
            square,
            square,
            vmem((8, 8, FACES), jnp.int32),
            vmem((12, 8, FACES), F32),
            vmem((SIDES, 8, FACES), jnp.int32),
            vmem((2, SIDES, HALO, FACES), F32),
            vmem((2, SIDES, HALO, FACES), F32),
            vmem((2, 8, FACES), F32),
            vmem((2, FACES), F32),
            vmem((2, FACES), F32),
            vmem((N_GY, 2, FACES), F32),
            vmem((N_GX, 2, FACES), F32),
            dma((2, SIDES)),
            dma((2, SIDES)),
            dma((4,)),
            pltpu.SemaphoreType.REGULAR((5,)),
        ],
        compiler_params=pltpu.CompilerParams(
            collective_id=collective_id, has_side_effects=True, vmem_limit_bytes=24 * 2**20
        ),
    )


PLANS = (
    (((1, 1, 2, 2), (3, 3, 4, 4)), 4, None),
    (((1, 2, 2, 3), (3, 4, 4, 5)), 5, None),
    (((1, 2, 3, 4), (5, 6, 7, 8)), 8, 0),
    (((1, 2, 3, 4), (5, 6, 7, 8)), 8, 1),
)


def body(rhs, inverse, weights, neighbours, send_lists, coloring):
    right = jnp.transpose(rhs, (1, 0, 2))
    plan, first, wide, halos = first_call(len(PLANS))(coloring, right, inverse[0], send_lists[0])
    solved, norms = lax.switch(
        plan[0, 0],
        [sweep_call(*choice, number) for number, choice in enumerate(PLANS)],
        coloring, right, first, wide, halos, weights[0], neighbours[0], send_lists[0],
    )
    return solved[None], norms[:, 0]


def solution(mesh):
    in_specs = (
        P("gx", None, "gy"),
        P("gx", None, None, "gy"),
        P("gx", None, "gy"),
        P("gx", None, "gy"),
        P("gx", None, "gy"),
        P("gx", "gy"),
    )
    out_specs = (P("gx", None, "gy"), P())
    return jax.shard_map(body, mesh=mesh, in_specs=in_specs, out_specs=out_specs, check_vma=False)
```
